512 devices in a mesh: mem: 2 (over x_lo), lat: 8 (over x_hi, y), lon: 32 (over z, core).
Axes of the slice: x: 4 (x_hi: 2, x_lo: 2; x = x_hi * 2 + x_lo), y: 4, z: 16, core: 2. Of those that a mesh axis runs over, the one named last changes fastest.
Arguments:
- members: float32 [2, 87, 64, 4096], P('mem', None, 'lat', 'lon'), may hold values from -6 to 6
- target: float32 [87, 64, 4096], P(None, 'lat', 'lon'), may hold values from -6 to 6
Outputs:
- gradient: float32 [2, 87, 64, 4096], P('mem', None, 'lat', 'lon')
- loss: float32 [], replicated
The draws below stay inside these ranges and needn't reach their ends.
All inputs are finite; a program needn't handle non-finite values.
Results may differ from the reference program's by a relative error of at most 0.0001.
Values sent between devices are 32-bit elements; how exact they have to be, the bound alone decides.
No kernel may reach another device: no remote copies, remote signals or barrier semaphores. Data moves between devices by JAX's collectives and lax.ppermute only.
A program may use at most 64 MiB of HBM per device.

```python
import jax
import jax.numpy as jnp
from jax import lax

C = 87
LEVELS = 7
NLAT = 64
NLON = 4096


def draw_fields(key, leading):
    row_index = jnp.arange(NLAT, dtype=jnp.float32)
    col_index = jnp.arange(NLON, dtype=jnp.float32)
    smooth = jnp.zeros(leading + (NLAT, NLON), jnp.float32)
    for wave in range(4):
        wave_key = jax.random.fold_in(key, 11 + wave)
        keys = jax.random.split(wave_key, 5)
        amplitude = 0.4 * jax.random.normal(keys[0], leading, jnp.float32)
        zonal = jax.random.randint(keys[1], leading, 1, 7).astype(jnp.float32)
        meridional = jax.random.uniform(keys[2], leading, jnp.float32, 0.5, 3.0)
        phase_lon = jax.random.uniform(keys[3], leading, jnp.float32, -jnp.pi, jnp.pi)
        phase_lat = jax.random.uniform(keys[4], leading, jnp.float32, -jnp.pi, jnp.pi)
        lon_wave = jnp.cos(2.0 * jnp.pi * zonal[..., None] * col_index / NLON + phase_lon[..., None])
        lat_wave = jnp.cos(jnp.pi * meridional[..., None] * row_index / NLAT + phase_lat[..., None])
        smooth = smooth + amplitude[..., None, None] * lat_wave[..., :, None] * lon_wave[..., None, :]
    scale_key = jax.random.fold_in(key, 31)
    channel_scale = jnp.exp(jax.random.uniform(scale_key, leading, jnp.float32, jnp.log(0.3), jnp.log(3.0)))
    rough_key = jax.random.fold_in(key, 41)
    rough = jnp.clip(jax.random.normal(rough_key, leading + (NLAT, NLON), jnp.float32), -3.5, 3.5)
    values = channel_scale[..., None, None] * (smooth + rough)
    return jnp.clip(values, -6.0, 6.0)


def draw_members(key, part):
    return draw_fields(jax.random.fold_in(key, 101), (2, C))


def draw_target(key, part):
    return draw_fields(jax.random.fold_in(key, 202), (C,))


def setup_inputs(seed: int = 0) -> dict:
    splits = jax.random.split(jax.random.key(seed), 3)
    return {
        "members": draw_members(jax.random.fold_in(splits[2], 71), 0),
        "target": draw_target(jax.random.fold_in(splits[2], 71), 0),
    }


smooth_eps = 0.05

def soft_abs(values):
    return jnp.sqrt(values * values + smooth_eps * smooth_eps)

def lat_weights(row_count):
    row_index = jnp.arange(row_count, dtype=jnp.float32)
    return jnp.cos((89.875 - 0.25 * row_index) * (jnp.pi / 180.0))

def box_weights():
    current = lat_weights(NLAT)
    boxes = [current]
    for level in range(LEVELS):
        reach = 2 ** level
        current = current + jnp.pad(current, (0, reach))[reach:reach + NLAT]
        boxes.append(current)
    return boxes

def rows_ahead(values, reach):
    widths = [(0, 0)] * (values.ndim - 2) + [(0, reach), (0, 0)]
    return jnp.pad(values, widths)[..., reach:reach + NLAT, :]

def channel_loss(pair, truth):
    boxes = box_weights()
    box_sum = boxes[0][:, None] * (pair - truth[None])
    loss_total = jnp.zeros((), jnp.float32)
    for scale in range(LEVELS + 1):
        if scale > 0:
            reach = 2 ** (scale - 1)
            box_sum = box_sum + rows_ahead(box_sum, reach)
            box_sum = box_sum + jnp.roll(box_sum, -reach, axis=-1)
        lat_box = boxes[scale]
        pooled = box_sum / (2.0 ** scale * lat_box)[:, None]
        leader = pooled[0]
        partner = pooled[1]
        score = 0.5 * (soft_abs(leader) + soft_abs(partner)) - 0.5 * soft_abs(leader - partner)
        loss_total = loss_total + jnp.sum(lat_box[:, None] * score) / (NLON * jnp.sum(lat_box))
    return loss_total

def reference(members, target):

    def per_channel(inputs):
        return jax.value_and_grad(channel_loss)(inputs[0], inputs[1])
    channel_values, channel_grads = lax.map(per_channel, (jnp.moveaxis(members, 1, 0), target))
    loss = jnp.sum(channel_values) / C
    gradient = jnp.moveaxis(channel_grads, 0, 1) * (NLAT * NLON)
    return (gradient, loss)
```

```python
import jax
import jax.numpy as jnp
import numpy as np
from jax import lax
from jax.experimental import pallas as pl
from jax.experimental.pallas import tpu as pltpu
from jax.sharding import Mesh, PartitionSpec as P

LEVELS = 7
EPS = 0.05
PLANE = ("mem", "lat")
LON = ("z", "core")


def box_vectors(row_count):
    row_index = np.arange(row_count, dtype=np.float32)
    degrees = np.float32(89.875) - np.float32(0.25) * row_index
    current = np.cos(degrees * np.float32(np.pi / 180.0)).astype(np.float32)
    boxes = [current]
    for level in range(LEVELS):
        reach = 2**level
        shifted = np.zeros_like(current)
        shifted[: max(row_count - reach, 0)] = current[reach:]
        current = current + shifted
        boxes.append(current)
    return boxes


def neighbour(value, by):
    count = lax.axis_size("z") * lax.axis_size("core")
    pairs = [(i, (i + by) % count) for i in range(count)]
    return lax.ppermute(value, LON, pairs)


def spread(value, axes):
    return lax.all_to_all(value, axes, 0, 0, tiled=True)


def box_kernel(loss_scale, grad_scale, channels, west_ref, own_ref, east_ref, eps_ref, weight_ref, grad_ref, cot_ref):
    peers, share = own_ref.shape[0], own_ref.shape[1]
    bands = peers // 2
    lane = lax.broadcasted_iota(jnp.int32, (8, 128), 1)
    row = lax.broadcasted_iota(jnp.int32, (8, 128), 0)
    zero = jnp.zeros((8, 128), jnp.float32)

    def rows_ahead(field, reach):
        if reach >= 8:
            hop = reach // 8
            return [field[b] + field[b + hop] if b + hop < bands else field[b] for b in range(bands)]
        rolled = [pltpu.roll(tile, 8 - reach, 0) for tile in field] + [zero]
        return [field[b] + jnp.where(row < 8 - reach, rolled[b], rolled[b + 1]) for b in range(bands)]

    def rows_behind(field, reach):
        if reach >= 8:
            hop = reach // 8
            return [field[b] + field[b - hop] if b >= hop else field[b] for b in range(bands)]
        rolled = [pltpu.roll(tile, reach, 0) for tile in field]
        before = [zero] + rolled[:-1]
        return [field[b] + jnp.where(row >= reach, rolled[b], before[b]) for b in range(bands)]

    def cols_ahead(west, own, east, reach, last):
        out = ([], [], [])
        for b in range(bands):
            rw, ro, re = (pltpu.roll(tile, 128 - reach, 1) for tile in (west[b], own[b], east[b]))
            out[0].append(west[b] + jnp.where(lane < 128 - reach, rw, ro))
            out[1].append(own[b] + jnp.where(lane < 128 - reach, ro, re))
            if not last:
                out[2].append(east[b] + re)
        return out

    def cols_behind(west, own, reach, last):
        out = ([], [])
        for b in range(bands):
            rw, ro = pltpu.roll(west[b], reach, 1), pltpu.roll(own[b], reach, 1)
            if not last:
                out[0].append(west[b] + rw)
            out[1].append(own[b] + jnp.where(lane >= reach, ro, rw))
        return out

    def evaluate(scale, first, second, band, side):
        eps = eps_ref[scale, band]
        apart = first - second
        t0, t1, td = first * first + eps, second * second + eps, apart * apart + eps
        r0, r1, rd = lax.rsqrt(t0), lax.rsqrt(t1), lax.rsqrt(td)
        away = apart * rd
        cot_ref[scale, 0, side, band] = (first * r0 - away) * grad_scale[scale]
        cot_ref[scale, 1, side, band] = (second * r1 + away) * grad_scale[scale]
        return t0 * r0 + t1 * r1 - td * rd

    def channel(c, total):
        fields = []
        for m in range(2):
            fields.append(
                [
                    [ref[m * bands + b, c] * weight_ref[b] for b in range(bands)]
                    for ref in (west_ref, own_ref, east_ref)
                ]
            )
        for scale in range(LEVELS + 1):
            if scale:
                reach = 2 ** (scale - 1)
                for m in range(2):
                    if reach < 8 * bands:
                        fields[m] = [rows_ahead(field, reach) for field in fields[m]]
                    fields[m] = cols_ahead(*fields[m], reach, scale == LEVELS)
            part = None
            for side in range(2):
                for b in range(bands):
                    term = evaluate(scale, fields[0][side][b], fields[1][side][b], b, side)
                    part = term if part is None else part + term
            total = total + part * loss_scale[scale]
        for m in range(2):
            adjoint = [[cot_ref[LEVELS, m, side, b] for b in range(bands)] for side in range(2)]
            for level in reversed(range(LEVELS)):
                reach = 2**level
                if reach < 8 * bands:
                    adjoint = [rows_behind(field, reach) for field in adjoint]
                west, own = cols_behind(*adjoint, reach, level == 0)
                if level:
                    west = [west[b] + cot_ref[level, m, 0, b] for b in range(bands)]
                own = [own[b] + cot_ref[level, m, 1, b] for b in range(bands)]
                adjoint = [west, own]
            for b in range(bands):
                grad_ref[m * bands + b, c] = adjoint[1][b] * weight_ref[b]
        return total

    first = (lax.axis_index("mem") * lax.axis_size("lat") + lax.axis_index("lat")) * share
    count = jnp.clip(channels - first, 0, share)
    total = lax.fori_loop(0, count, channel, zero)
    for p in range(peers):
        grad_ref[p, share] = total


def shards(members, target):
    channels, row_count, col_count = target.shape
    bands = lax.axis_size("lat")
    peers = lax.axis_size("mem") * bands
    nlat, nlon = row_count * bands, col_count * lax.axis_size("z") * lax.axis_size("core")
    share = -(-channels // peers)
    boxes = box_vectors(nlat)
    totals = [float(np.sum(vector, dtype=np.float64)) for vector in boxes]
    loss_scale = [0.5 / (2.0**s * channels * nlon * totals[s]) for s in range(LEVELS + 1)]
    grad_scale = [0.5 * nlat / (2.0**s * totals[s]) for s in range(LEVELS + 1)]
    eps = np.stack([(np.float32(2.0**s * EPS) * boxes[s]) ** 2 for s in range(LEVELS + 1)])
    eps = np.broadcast_to(eps.reshape(LEVELS + 1, bands, 8, 1), (LEVELS + 1, bands, 8, 128))
    weight = np.broadcast_to(boxes[0].reshape(bands, 8, 1), (bands, 8, 128))

    apart = jnp.pad(members[0] - target, ((0, peers * share - channels), (0, 0), (0, 0)))
    own = spread(apart, PLANE).reshape(peers, share, row_count, col_count)
    east, west = neighbour(own, -1), neighbour(own, 1)
    vmem = pl.BlockSpec(memory_space=pltpu.VMEM)

    def kernel(*refs):
        box_kernel(loss_scale, grad_scale, channels, *refs)

    grad = pl.pallas_call(
        kernel,
        out_shape=jax.ShapeDtypeStruct((peers, share + 1, row_count, col_count), jnp.float32),
        in_specs=[vmem] * 5,
        out_specs=vmem,
        scratch_shapes=[pltpu.VMEM((LEVELS + 1, 2, 2, bands, 8, 128), jnp.float32)],
        name="boxes",
    )(west, own, east, jnp.asarray(eps), jnp.asarray(weight))
    back = spread(grad, PLANE)
    plane_loss = jnp.sum(back[:, share], axis=0)
    all_loss = spread(jnp.broadcast_to(plane_loss[None], (lax.axis_size("z"), 8, 128)), ("z",))
    gradient = back[:, :share].reshape(1, peers * share, row_count, col_count)[:, :channels]
    return gradient, jnp.sum(all_loss)


def solution(mesh):
    grid = mesh.devices
    fine = Mesh(grid.reshape(*grid.shape[:2], grid.shape[2] // 2, 2), ("mem", "lat", "z", "core"))
    spec = P("mem", None, "lat", LON)
    return jax.shard_map(
        shards,
        mesh=fine,
        in_specs=(spec, P(None, "lat", LON)),
        out_specs=(spec, P()),
        check_vma=False,
    )
```

```python
import functools

import jax
import jax.numpy as jnp
import numpy as np
from jax import lax
from jax.experimental import pallas as pl
from jax.experimental.pallas import tpu as pltpu
from jax.sharding import Mesh, PartitionSpec as P

LEVELS = 7
EPS = 0.05
GROUPS = (3, 3)
PLANE = ("mem", "lat")
LON = ("z", "core")


def box_vectors(row_count):
    row_index = np.arange(row_count, dtype=np.float32)
    degrees = np.float32(89.875) - np.float32(0.25) * row_index
    current = np.cos(degrees * np.float32(np.pi / 180.0)).astype(np.float32)
    boxes = [current]
    for level in range(LEVELS):
        reach = 2**level
        shifted = np.zeros_like(current)
        shifted[: max(row_count - reach, 0)] = current[reach:]
        current = current + shifted
        boxes.append(current)
    return boxes


def neighbour(value, by):
    count = lax.axis_size("z") * lax.axis_size("core")
    pairs = [(i, (i + by) % count) for i in range(count)]
    return lax.ppermute(value, LON, pairs)


def spread(value, axes):
    return lax.all_to_all(value, axes, 0, 0, tiled=True)


def box_kernel(loss_scale, grad_scale, channels, start, final, west_ref, own_ref, east_ref, table_ref, *refs):
    grad_ref, eps_ref, weight_ref, cot_ref = refs[-4:]
    peers, share, group = own_ref.shape[0], own_ref.shape[1], west_ref.shape[1]
    bands = peers // 2
    for b in range(bands):
        table = table_ref[b]
        for scale in range(LEVELS + 1):
            eps_ref[scale, b] = jnp.broadcast_to(table[:, scale : scale + 1], (8, 128))
        weight_ref[b] = jnp.broadcast_to(table[:, LEVELS + 1 : LEVELS + 2], (8, 128))
    lane = lax.broadcasted_iota(jnp.int32, (8, 128), 1)
    row = lax.broadcasted_iota(jnp.int32, (8, 128), 0)
    zero = jnp.zeros((8, 128), jnp.float32)

    def rows_ahead(field, reach):
        if reach >= 8:
            hop = reach // 8
            return [field[b] + field[b + hop] if b + hop < bands else field[b] for b in range(bands)]
        rolled = [pltpu.roll(tile, 8 - reach, 0) for tile in field] + [zero]
        return [field[b] + jnp.where(row < 8 - reach, rolled[b], rolled[b + 1]) for b in range(bands)]

    def rows_behind(field, reach):
        if reach >= 8:
            hop = reach // 8
            return [field[b] + field[b - hop] if b >= hop else field[b] for b in range(bands)]
        rolled = [pltpu.roll(tile, reach, 0) for tile in field]
        before = [zero] + rolled[:-1]
        return [field[b] + jnp.where(row >= reach, rolled[b], before[b]) for b in range(bands)]

    def cols_ahead(west, own, east, reach, last):
        out = ([], [], [])
        for b in range(bands):
            rw, ro, re = (pltpu.roll(tile, 128 - reach, 1) for tile in (west[b], own[b], east[b]))
            out[0].append(west[b] + jnp.where(lane < 128 - reach, rw, ro))
            out[1].append(own[b] + jnp.where(lane < 128 - reach, ro, re))
            if not last:
                out[2].append(east[b] + re)
        return out

    def cols_behind(west, own, reach, last):
        out = ([], [])
        for b in range(bands):
            rw, ro = pltpu.roll(west[b], reach, 1), pltpu.roll(own[b], reach, 1)
            if not last:
                out[0].append(west[b] + rw)
            out[1].append(own[b] + jnp.where(lane >= reach, ro, rw))
        return out

    def evaluate(scale, first, second, band, side):
        eps = eps_ref[scale, band]
        apart = first - second
        t0, t1, td = first * first + eps, second * second + eps, apart * apart + eps
        r0, r1, rd = lax.rsqrt(t0), lax.rsqrt(t1), lax.rsqrt(td)
        away = apart * rd
        cot_ref[scale, 0, side, band] = (first * r0 - away) * grad_scale[scale]
        cot_ref[scale, 1, side, band] = (second * r1 + away) * grad_scale[scale]
        return t0 * r0 + t1 * r1 - td * rd

    def channel(c, total):
        fields = []
        for m in range(2):
            fields.append(
                [
                    [ref[m * bands + b, c + first] * weight_ref[b] for b in range(bands)]
                    for ref, first in ((west_ref, 0), (own_ref, start), (east_ref, 0))
                ]
            )
        for scale in range(LEVELS + 1):
            if scale:
                reach = 2 ** (scale - 1)
                for m in range(2):
                    if reach < 8 * bands:
                        fields[m] = [rows_ahead(field, reach) for field in fields[m]]
                    fields[m] = cols_ahead(*fields[m], reach, scale == LEVELS)
            part = None
            for side in range(2):
                for b in range(bands):
                    term = evaluate(scale, fields[0][side][b], fields[1][side][b], b, side)
                    part = term if part is None else part + term
            total = total + part * loss_scale[scale]
        for m in range(2):
            adjoint = [[cot_ref[LEVELS, m, side, b] for b in range(bands)] for side in range(2)]
            for level in reversed(range(LEVELS)):
                reach = 2**level
                if reach < 8 * bands:
                    adjoint = [rows_behind(field, reach) for field in adjoint]
                west, own = cols_behind(*adjoint, reach, level == 0)
                if level:
                    west = [west[b] + cot_ref[level, m, 0, b] for b in range(bands)]
                own = [own[b] + cot_ref[level, m, 1, b] for b in range(bands)]
                adjoint = [west, own]
            for b in range(bands):
                grad_ref[m * bands + b, c + start] = adjoint[1][b] * weight_ref[b]
        return total

    first = (lax.axis_index("mem") * lax.axis_size("lat") + lax.axis_index("lat")) * share + start
    count = jnp.clip(channels - first, 0, group)
    total = lax.fori_loop(0, count, channel, zero if start == 0 else refs[0][0, share])
    for p in range(peers if final else 1):
        grad_ref[p, share] = total


def shards(members, target):
    channels, row_count, col_count = target.shape
    bands = lax.axis_size("lat")
    peers = lax.axis_size("mem") * bands
    nlat, nlon = row_count * bands, col_count * lax.axis_size("z") * lax.axis_size("core")
    share = -(-channels // peers)
    boxes = box_vectors(nlat)
    totals = [float(np.sum(vector, dtype=np.float64)) for vector in boxes]
    loss_scale = [0.5 / (2.0**s * channels * nlon * totals[s]) for s in range(LEVELS + 1)]
    grad_scale = [0.5 * nlat / (2.0**s * totals[s]) for s in range(LEVELS + 1)]
    table = np.zeros((bands, 8, 128), np.float32)
    for s in range(LEVELS + 1):
        table[:, :, s] = ((np.float32(2.0**s * EPS) * boxes[s]) ** 2).reshape(bands, 8)
    table[:, :, LEVELS + 1] = boxes[0].reshape(bands, 8)

    apart = jnp.pad(members[0] - target, ((0, peers * share - channels), (0, 0), (0, 0)))
    own = spread(apart, PLANE).reshape(peers, share, row_count, col_count)
    vmem = pl.BlockSpec(memory_space=pltpu.VMEM)
    grad = None
    halos = []
    start = 0
    for size in GROUPS:
        part = own[:, start : start + size]
        halos.append((start, size, neighbour(part, 1), neighbour(part, -1)))
        start += size
    for start, size, west, east in halos:
        grad = pl.pallas_call(
            functools.partial(box_kernel, loss_scale, grad_scale, channels, start, start + size == share),
            out_shape=jax.ShapeDtypeStruct((peers, share + 1, row_count, col_count), jnp.float32),
            in_specs=[vmem] * (4 if start == 0 else 5),
            out_specs=vmem,
            input_output_aliases={} if start == 0 else {4: 0},
            scratch_shapes=[
                pltpu.VMEM((LEVELS + 1, bands, 8, 128), jnp.float32),
                pltpu.VMEM((bands, 8, 128), jnp.float32),
                pltpu.VMEM((LEVELS + 1, 2, 2, bands, 8, 128), jnp.float32),
            ],
            compiler_params=pltpu.CompilerParams(vmem_limit_bytes=16 << 20),
            name=f"boxes_{start}",
        )(west, own, east, jnp.asarray(table), *(() if start == 0 else (grad,)))
    back = spread(grad, PLANE)
    plane_loss = jnp.sum(back[:, share], axis=(0, 1))
    all_loss = spread(jnp.broadcast_to(plane_loss, (lax.axis_size("z"), 1, col_count)), ("z",))
    gradient = back[:, :share].reshape(1, peers * share, row_count, col_count)[:, :channels]
    return gradient, jnp.sum(all_loss)


def solution(mesh):
    grid = mesh.devices
    fine = Mesh(grid.reshape(*grid.shape[:2], grid.shape[2] // 2, 2), ("mem", "lat", "z", "core"))
    spec = P("mem", None, "lat", LON)
    return jax.shard_map(
        shards,
        mesh=fine,
        in_specs=(spec, P(None, "lat", LON)),
        out_specs=(spec, P()),
        check_vma=False,
    )
```

```python
import functools
import math

import jax
import jax.numpy as jnp
import numpy as np
from jax import lax
from jax.experimental import pallas as pl
from jax.experimental.pallas import tpu as pltpu
from jax.sharding import Mesh, PartitionSpec as P

LEVELS = 7
EPS = 0.05
GROUPS = (3, 3)
FIRST_PLANE = 14
FIRST_Z = 8
PLANE = ("mem", "lat")
LON = ("z", "core")


def box_vectors(row_count):
    row_index = np.arange(row_count, dtype=np.float32)
    degrees = np.float32(89.875) - np.float32(0.25) * row_index
    current = np.cos(degrees * np.float32(np.pi / 180.0)).astype(np.float32)
    boxes = [current]
    for level in range(LEVELS):
        reach = 2**level
        shifted = np.zeros_like(current)
        shifted[: max(row_count - reach, 0)] = current[reach:]
        current = current + shifted
        boxes.append(current)
    return boxes


def neighbour(value, by):
    count = lax.axis_size("z") * lax.axis_size("core")
    pairs = [(i, (i + by) % count) for i in range(count)]
    return lax.ppermute(value, LON, pairs)


def turned(count, first):
    return [(first + i) % count for i in range(count)]


def spread(value, axes, first):
    order = turned(math.prod(lax.axis_size(axis) for axis in axes), first)
    axes = axes if len(axes) > 1 else axes[0]
    return lax.all_to_all(value, axes, 0, 0, axis_index_groups=[order] if first else None, tiled=True)


def box_kernel(loss_scale, grad_scale, channels, start, final, west_ref, own_ref, east_ref, table_ref, *refs):
    grad_ref, eps_ref, weight_ref, cot_ref = refs[-4:]
    peers, share, group = own_ref.shape[0], own_ref.shape[1], west_ref.shape[1]
    bands = peers // 2
    for b in range(bands):
        table = table_ref[b]
        for scale in range(LEVELS + 1):
            eps_ref[scale, b] = jnp.broadcast_to(table[:, scale : scale + 1], (8, 128))
        weight_ref[b] = jnp.broadcast_to(table[:, LEVELS + 1 : LEVELS + 2], (8, 128))
    lane = lax.broadcasted_iota(jnp.int32, (8, 128), 1)
    row = lax.broadcasted_iota(jnp.int32, (8, 128), 0)
    zero = jnp.zeros((8, 128), jnp.float32)

    def rows_ahead(field, reach):
        if reach >= 8:
            hop = reach // 8
            return [field[b] + field[b + hop] if b + hop < bands else field[b] for b in range(bands)]
        rolled = [pltpu.roll(tile, 8 - reach, 0) for tile in field] + [zero]
        return [field[b] + jnp.where(row < 8 - reach, rolled[b], rolled[b + 1]) for b in range(bands)]

    def rows_behind(field, reach):
        if reach >= 8:
            hop = reach // 8
            return [field[b] + field[b - hop] if b >= hop else field[b] for b in range(bands)]
        rolled = [pltpu.roll(tile, reach, 0) for tile in field]
        before = [zero] + rolled[:-1]
        return [field[b] + jnp.where(row >= reach, rolled[b], before[b]) for b in range(bands)]

    def cols_ahead(west, own, east, reach, last):
        out = ([], [], [])
        for b in range(bands):
            rw, ro, re = (pltpu.roll(tile, 128 - reach, 1) for tile in (west[b], own[b], east[b]))
            out[0].append(west[b] + jnp.where(lane < 128 - reach, rw, ro))
            out[1].append(own[b] + jnp.where(lane < 128 - reach, ro, re))
            if not last:
                out[2].append(east[b] + re)
        return out

    def cols_behind(west, own, reach, last):
        out = ([], [])
        for b in range(bands):
            rw, ro = pltpu.roll(west[b], reach, 1), pltpu.roll(own[b], reach, 1)
            if not last:
                out[0].append(west[b] + rw)
            out[1].append(own[b] + jnp.where(lane >= reach, ro, rw))
        return out

    def evaluate(scale, first, second, band, side):
        eps = eps_ref[scale, band]
        apart = first - second
        t0, t1, td = first * first + eps, second * second + eps, apart * apart + eps
        r0, r1, rd = lax.rsqrt(t0), lax.rsqrt(t1), lax.rsqrt(td)
        away = apart * rd
        cot_ref[scale, 0, side, band] = (first * r0 - away) * grad_scale[scale]
        cot_ref[scale, 1, side, band] = (second * r1 + away) * grad_scale[scale]
        return t0 * r0 + t1 * r1 - td * rd

    def channel(c, total):
        fields = []
        for m in range(2):
            fields.append(
                [
                    [ref[(m * bands + b - FIRST_PLANE) % peers, c + skip] * weight_ref[b] for b in range(bands)]
                    for ref, skip in ((west_ref, 0), (own_ref, start), (east_ref, 0))
                ]
            )
        for scale in range(LEVELS + 1):
            if scale:
                reach = 2 ** (scale - 1)
                for m in range(2):
                    if reach < 8 * bands:
                        fields[m] = [rows_ahead(field, reach) for field in fields[m]]
                    fields[m] = cols_ahead(*fields[m], reach, scale == LEVELS)
            part = None
            for side in range(2):
                for b in range(bands):
                    term = evaluate(scale, fields[0][side][b], fields[1][side][b], b, side)
                    part = term if part is None else part + term
            total = total + part * loss_scale[scale]
        for m in range(2):
            adjoint = [[cot_ref[LEVELS, m, side, b] for b in range(bands)] for side in range(2)]
            for level in reversed(range(LEVELS)):
                reach = 2**level
                if reach < 8 * bands:
                    adjoint = [rows_behind(field, reach) for field in adjoint]
                west, own = cols_behind(*adjoint, reach, level == 0)
                if level:
                    west = [west[b] + cot_ref[level, m, 0, b] for b in range(bands)]
                own = [own[b] + cot_ref[level, m, 1, b] for b in range(bands)]
                adjoint = [west, own]
            for b in range(bands):
                grad_ref[(m * bands + b - FIRST_PLANE) % peers, c + start] = adjoint[1][b] * weight_ref[b]
        return total

    me = lax.axis_index("mem") * lax.axis_size("lat") + lax.axis_index("lat")
    place = lax.rem(me + (peers - FIRST_PLANE), peers)
    count = jnp.clip(channels - place * share - start, 0, group)
    total = lax.fori_loop(0, count, channel, zero if start == 0 else refs[0][0, share])
    for p in range(peers if final else 1):
        grad_ref[p, share] = total


def shards(members, target):
    channels, row_count, col_count = target.shape
    bands = lax.axis_size("lat")
    peers = lax.axis_size("mem") * bands
    nlat, nlon = row_count * bands, col_count * lax.axis_size("z") * lax.axis_size("core")
    share = -(-channels // peers)
    boxes = box_vectors(nlat)
    totals = [float(np.sum(vector, dtype=np.float64)) for vector in boxes]
    loss_scale = [0.5 / (2.0**s * channels * nlon * totals[s]) for s in range(LEVELS + 1)]
    grad_scale = [0.5 * nlat / (2.0**s * totals[s]) for s in range(LEVELS + 1)]
    table = np.zeros((bands, 8, 128), np.float32)
    for s in range(LEVELS + 1):
        table[:, :, s] = ((np.float32(2.0**s * EPS) * boxes[s]) ** 2).reshape(bands, 8)
    table[:, :, LEVELS + 1] = boxes[0].reshape(bands, 8)

    apart = jnp.pad(members[0] - target, ((0, peers * share - channels), (0, 0), (0, 0)))
    own = spread(apart, PLANE, FIRST_PLANE).reshape(peers, share, row_count, col_count)
    vmem = pl.BlockSpec(memory_space=pltpu.VMEM)
    grad = None
    halos = []
    start = 0
    for size in GROUPS:
        part = own[:, start : start + size]
        halos.append((start, size, neighbour(part, 1), neighbour(part, -1)))
        start += size
    for start, size, west, east in halos:
        grad = pl.pallas_call(
            functools.partial(box_kernel, loss_scale, grad_scale, channels, start, start + size == share),
            out_shape=jax.ShapeDtypeStruct((peers, share + 1, row_count, col_count), jnp.float32),
            in_specs=[vmem] * (4 if start == 0 else 5),
            out_specs=vmem,
            input_output_aliases={} if start == 0 else {4: 0},
            scratch_shapes=[
                pltpu.VMEM((LEVELS + 1, bands, 8, 128), jnp.float32),
                pltpu.VMEM((bands, 8, 128), jnp.float32),
                pltpu.VMEM((LEVELS + 1, 2, 2, bands, 8, 128), jnp.float32),
            ],
            compiler_params=pltpu.CompilerParams(vmem_limit_bytes=16 << 20),
            name=f"boxes_{start}",
        )(west, own, east, jnp.asarray(table), *(() if start == 0 else (grad,)))
    back = spread(grad, PLANE, FIRST_PLANE)
    plane_loss = jnp.sum(back[:, share], axis=(0, 1))
    all_loss = spread(jnp.broadcast_to(plane_loss, (lax.axis_size("z"), 1, col_count)), ("z",), FIRST_Z)
    gradient = back[:, :share].reshape(1, peers * share, row_count, col_count)[:, :channels]
    return gradient, jnp.sum(all_loss)


def solution(mesh):
    grid = mesh.devices
    fine = Mesh(grid.reshape(*grid.shape[:2], grid.shape[2] // 2, 2), ("mem", "lat", "z", "core"))
    spec = P("mem", None, "lat", LON)
    return jax.shard_map(
        shards,
        mesh=fine,
        in_specs=(spec, P(None, "lat", LON)),
        out_specs=(spec, P()),
        check_vma=False,
    )
```

```python
import functools
import math

import jax
import jax.numpy as jnp
import numpy as np
from jax import lax
from jax.experimental import pallas as pl
from jax.experimental.pallas import tpu as pltpu
from jax.sharding import Mesh, PartitionSpec as P

LEVELS = 7
EPS = 0.05
GROUPS = (3, 3)
FIRST_PLANE = 14
FIRST_Z = 8
PLANE = ("mem", "lat")
LON = ("z", "core")


def box_vectors(row_count):
    row_index = np.arange(row_count, dtype=np.float32)
    degrees = np.float32(89.875) - np.float32(0.25) * row_index
    current = np.cos(degrees * np.float32(np.pi / 180.0)).astype(np.float32)
    boxes = [current]
    for level in range(LEVELS):
        reach = 2**level
        shifted = np.zeros_like(current)
        shifted[: max(row_count - reach, 0)] = current[reach:]
        current = current + shifted
        boxes.append(current)
    return boxes


def neighbour(value, by):
    count = lax.axis_size("z") * lax.axis_size("core")
    pairs = [(i, (i + by) % count) for i in range(count)]
    return lax.ppermute(value, LON, pairs)


def turned(count, first):
    return [(first + i) % count for i in range(count)]


def spread(value, axes, first):
    order = turned(math.prod(lax.axis_size(axis) for axis in axes), first)
    axes = axes if len(axes) > 1 else axes[0]
    return lax.all_to_all(value, axes, 0, 0, axis_index_groups=[order] if first else None, tiled=True)


def box_kernel(loss_scale, grad_scale, channels, start, final, west_ref, own_ref, east_ref, table_ref, *refs):
    eps_ref, weight_ref, cot_ref = refs[-3:]
    grad_ref, term_ref = refs[-5:-3] if final else (refs[-4], None)
    peers, share, group = own_ref.shape[0], own_ref.shape[1], west_ref.shape[1]
    bands = peers // 2
    for b in range(bands):
        table = table_ref[b]
        for scale in range(LEVELS + 1):
            eps_ref[scale, b] = jnp.broadcast_to(table[:, scale : scale + 1], (8, 128))
        weight_ref[b] = jnp.broadcast_to(table[:, LEVELS + 1 : LEVELS + 2], (8, 128))
    lane = lax.broadcasted_iota(jnp.int32, (8, 128), 1)
    row = lax.broadcasted_iota(jnp.int32, (8, 128), 0)
    zero = jnp.zeros((8, 128), jnp.float32)

    def rows_ahead(field, reach):
        if reach >= 8:
            hop = reach // 8
            return [field[b] + field[b + hop] if b + hop < bands else field[b] for b in range(bands)]
        rolled = [pltpu.roll(tile, 8 - reach, 0) for tile in field] + [zero]
        return [field[b] + jnp.where(row < 8 - reach, rolled[b], rolled[b + 1]) for b in range(bands)]

    def rows_behind(field, reach):
        if reach >= 8:
            hop = reach // 8
            return [field[b] + field[b - hop] if b >= hop else field[b] for b in range(bands)]
        rolled = [pltpu.roll(tile, reach, 0) for tile in field]
        before = [zero] + rolled[:-1]
        return [field[b] + jnp.where(row >= reach, rolled[b], before[b]) for b in range(bands)]

    def cols_ahead(west, own, east, reach, last):
        out = ([], [], [])
        for b in range(bands):
            rw, ro, re = (pltpu.roll(tile, 128 - reach, 1) for tile in (west[b], own[b], east[b]))
            out[0].append(west[b] + jnp.where(lane < 128 - reach, rw, ro))
            out[1].append(own[b] + jnp.where(lane < 128 - reach, ro, re))
            if not last:
                out[2].append(east[b] + re)
        return out

    def cols_behind(west, own, reach, last):
        out = ([], [])
        for b in range(bands):
            rw, ro = pltpu.roll(west[b], reach, 1), pltpu.roll(own[b], reach, 1)
            if not last:
                out[0].append(west[b] + rw)
            out[1].append(own[b] + jnp.where(lane >= reach, ro, rw))
        return out

    def evaluate(scale, first, second, band, side):
        eps = eps_ref[scale, band]
        apart = first - second
        t0, t1, td = first * first + eps, second * second + eps, apart * apart + eps
        r0, r1, rd = lax.rsqrt(t0), lax.rsqrt(t1), lax.rsqrt(td)
        away = apart * rd
        cot_ref[scale, 0, side, band] = (first * r0 - away) * grad_scale[scale]
        cot_ref[scale, 1, side, band] = (second * r1 + away) * grad_scale[scale]
        return t0 * r0 + t1 * r1 - td * rd

    def channel(c, total):
        fields = []
        for m in range(2):
            fields.append(
                [
                    [ref[(m * bands + b - FIRST_PLANE) % peers, c + skip] * weight_ref[b] for b in range(bands)]
                    for ref, skip in ((west_ref, 0), (own_ref, start), (east_ref, 0))
                ]
            )
        for scale in range(LEVELS + 1):
            if scale:
                reach = 2 ** (scale - 1)
                for m in range(2):
                    if reach < 8 * bands:
                        fields[m] = [rows_ahead(field, reach) for field in fields[m]]
                    fields[m] = cols_ahead(*fields[m], reach, scale == LEVELS)
            part = None
            for side in range(2):
                for b in range(bands):
                    term = evaluate(scale, fields[0][side][b], fields[1][side][b], b, side)
                    part = term if part is None else part + term
            total = total + part * loss_scale[scale]
        for m in range(2):
            adjoint = [[cot_ref[LEVELS, m, side, b] for b in range(bands)] for side in range(2)]
            for level in reversed(range(LEVELS)):
                reach = 2**level
                if reach < 8 * bands:
                    adjoint = [rows_behind(field, reach) for field in adjoint]
                west, own = cols_behind(*adjoint, reach, level == 0)
                if level:
                    west = [west[b] + cot_ref[level, m, 0, b] for b in range(bands)]
                own = [own[b] + cot_ref[level, m, 1, b] for b in range(bands)]
                adjoint = [west, own]
            for b in range(bands):
                grad_ref[(m * bands + b - FIRST_PLANE) % peers, c + start] = adjoint[1][b] * weight_ref[b]
        return total

    me = lax.axis_index("mem") * lax.axis_size("lat") + lax.axis_index("lat")
    place = lax.rem(me + (peers - FIRST_PLANE), peers)
    count = jnp.clip(channels - place * share - start, 0, group)
    total = lax.fori_loop(0, count, channel, zero if start == 0 else refs[0][0, share])
    if final:
        term_ref[...] = jnp.broadcast_to(jnp.sum(total, axis=0).reshape(1, 1, 128), term_ref.shape)
    else:
        grad_ref[0, share] = total


def add_kernel(terms_ref, _, grad_ref):
    total = jnp.sum(terms_ref[...], axis=0)
    share = grad_ref.shape[1] - 1
    for p in range(grad_ref.shape[0]):
        grad_ref[p, share, 0:1] = total


def end_kernel(back_ref, gradient_ref, loss_ref, sum_ref, sems):
    peers, share, channels = back_ref.shape[0], back_ref.shape[1] - 1, gradient_ref.shape[0]
    copies = []
    for p in range(peers):
        size = min(share, channels - p * share)
        if size > 0:
            copies.append(
                pltpu.make_async_copy(
                    back_ref.at[p, pl.ds(0, size)], gradient_ref.at[pl.ds(p * share, size)], sems.at[p]
                )
            )
    for copy in copies:
        copy.start()
    total = back_ref[0, share, 0:1]
    for p in range(1, peers):
        total = total + back_ref[p, share, 0:1]
    sum_ref[...] = jnp.broadcast_to(jnp.sum(total, axis=1, keepdims=True), sum_ref.shape)
    copies.append(pltpu.make_async_copy(sum_ref, loss_ref, sems.at[peers]))
    copies[-1].start()
    for copy in copies:
        copy.wait()


def shards(members, target):
    channels, row_count, col_count = target.shape
    bands = lax.axis_size("lat")
    peers = lax.axis_size("mem") * bands
    nlat, nlon = row_count * bands, col_count * lax.axis_size("z") * lax.axis_size("core")
    share = -(-channels // peers)
    boxes = box_vectors(nlat)
    totals = [float(np.sum(vector, dtype=np.float64)) for vector in boxes]
    loss_scale = [0.5 / (2.0**s * channels * nlon * totals[s]) for s in range(LEVELS + 1)]
    grad_scale = [0.5 * nlat / (2.0**s * totals[s]) for s in range(LEVELS + 1)]
    table = np.zeros((bands, 8, 128), np.float32)
    for s in range(LEVELS + 1):
        table[:, :, s] = ((np.float32(2.0**s * EPS) * boxes[s]) ** 2).reshape(bands, 8)
    table[:, :, LEVELS + 1] = boxes[0].reshape(bands, 8)

    apart = jnp.pad(members[0] - target, ((0, peers * share - channels), (0, 0), (0, 0)))
    own = spread(apart, PLANE, FIRST_PLANE).reshape(peers, share, row_count, col_count)
    vmem = pl.BlockSpec(memory_space=pltpu.VMEM)
    shapes = [
        jax.ShapeDtypeStruct((peers, share + 1, row_count, col_count), jnp.float32),
        jax.ShapeDtypeStruct((lax.axis_size("z"), 1, col_count), jnp.float32),
    ]
    grad = None
    halos = []
    start = 0
    for size in GROUPS:
        part = own[:, start : start + size]
        halos.append((start, size, neighbour(part, 1), neighbour(part, -1)))
        start += size
    for start, size, west, east in halos:
        grad, *term = pl.pallas_call(
            functools.partial(box_kernel, loss_scale, grad_scale, channels, start, start + size == share),
            out_shape=shapes if start + size == share else shapes[:1],
            in_specs=[vmem] * (4 if start == 0 else 5),
            out_specs=[vmem] * (2 if start + size == share else 1),
            input_output_aliases={} if start == 0 else {4: 0},
            scratch_shapes=[
                pltpu.VMEM((LEVELS + 1, bands, 8, 128), jnp.float32),
                pltpu.VMEM((bands, 8, 128), jnp.float32),
                pltpu.VMEM((LEVELS + 1, 2, 2, bands, 8, 128), jnp.float32),
            ],
            compiler_params=pltpu.CompilerParams(vmem_limit_bytes=16 << 20),
            name=f"boxes_{start}",
        )(west, own, east, jnp.asarray(table), *(() if start == 0 else (grad,)))
    terms = spread(term[0], ("z",), FIRST_Z)
    grad = pl.pallas_call(
        add_kernel,
        out_shape=jax.ShapeDtypeStruct(grad.shape, jnp.float32),
        in_specs=[vmem, vmem],
        out_specs=vmem,
        input_output_aliases={1: 0},
        compiler_params=pltpu.CompilerParams(vmem_limit_bytes=4 << 20),
        name="add_terms",
    )(terms, grad)
    back = spread(grad, PLANE, FIRST_PLANE)
    gradient, loss = pl.pallas_call(
        end_kernel,
        out_shape=(
            jax.ShapeDtypeStruct((channels, row_count, col_count), jnp.float32),
            jax.ShapeDtypeStruct((1, 128), jnp.float32),
        ),
        in_specs=[vmem],
        out_specs=(pl.BlockSpec(memory_space=pl.ANY), pl.BlockSpec(memory_space=pl.ANY)),
        scratch_shapes=[pltpu.VMEM((1, 128), jnp.float32), pltpu.SemaphoreType.DMA((peers + 1,))],
        compiler_params=pltpu.CompilerParams(vmem_limit_bytes=4 << 20),
        name="end",
    )(back)
    return gradient[None], loss[0, 0]


def solution(mesh):
    grid = mesh.devices
    fine = Mesh(grid.reshape(*grid.shape[:2], grid.shape[2] // 2, 2), ("mem", "lat", "z", "core"))
    spec = P("mem", None, "lat", LON)
    return jax.shard_map(
        shards,
        mesh=fine,
        in_specs=(spec, P(None, "lat", LON)),
        out_specs=(spec, P()),
        check_vma=False,
    )
```

```python
import functools
import math

import jax
import jax.numpy as jnp
import numpy as np
from jax import lax
from jax.experimental import pallas as pl
from jax.experimental.pallas import tpu as pltpu
from jax.sharding import Mesh, PartitionSpec as P

LEVELS = 7
EPS = 0.05
GROUPS = (4, 2)
FIRST_PLANE = 14
FIRST_Z = 8
PLANE = ("mem", "lat")
LON = ("z", "core")


def box_vectors(row_count):
    row_index = np.arange(row_count, dtype=np.float32)
    degrees = np.float32(89.875) - np.float32(0.25) * row_index
    current = np.cos(degrees * np.float32(np.pi / 180.0)).astype(np.float32)
    boxes = [current]
    for level in range(LEVELS):
        reach = 2**level
        shifted = np.zeros_like(current)
        shifted[: max(row_count - reach, 0)] = current[reach:]
        current = current + shifted
        boxes.append(current)
    return boxes


def neighbour(value, by):
    count = lax.axis_size("z") * lax.axis_size("core")
    pairs = [(i, (i + by) % count) for i in range(count)]
    return lax.ppermute(value, LON, pairs)


def turned(count, first):
    return [(first + i) % count for i in range(count)]


def spread(value, axes, first):
    order = turned(math.prod(lax.axis_size(axis) for axis in axes), first)
    axes = axes if len(axes) > 1 else axes[0]
    return lax.all_to_all(value, axes, 0, 0, axis_index_groups=[order] if first else None, tiled=True)


def box_kernel(loss_scale, grad_scale, channels, start, final, west_ref, own_ref, east_ref, table_ref, *refs):
    eps_ref, weight_ref, cot_ref = refs[-3:]
    grad_ref, term_ref = refs[-5:-3] if final else (refs[-4], None)
    peers, share, group = own_ref.shape[0], own_ref.shape[1], west_ref.shape[1]
    bands = peers // 2
    for b in range(bands):
        table = table_ref[b]
        for scale in range(LEVELS + 1):
            eps_ref[scale, b] = jnp.broadcast_to(table[:, scale : scale + 1], (8, 128))
        weight_ref[b] = jnp.broadcast_to(table[:, LEVELS + 1 : LEVELS + 2], (8, 128))
    lane = lax.broadcasted_iota(jnp.int32, (8, 128), 1)
    row = lax.broadcasted_iota(jnp.int32, (8, 128), 0)
    zero = jnp.zeros((8, 128), jnp.float32)

    def rows_ahead(field, reach):
        if reach >= 8:
            hop = reach // 8
            return [field[b] + field[b + hop] if b + hop < bands else field[b] for b in range(bands)]
        rolled = [pltpu.roll(tile, 8 - reach, 0) for tile in field] + [zero]
        return [field[b] + jnp.where(row < 8 - reach, rolled[b], rolled[b + 1]) for b in range(bands)]

    def rows_behind(field, reach):
        if reach >= 8:
            hop = reach // 8
            return [field[b] + field[b - hop] if b >= hop else field[b] for b in range(bands)]
        rolled = [pltpu.roll(tile, reach, 0) for tile in field]
        before = [zero] + rolled[:-1]
        return [field[b] + jnp.where(row >= reach, rolled[b], before[b]) for b in range(bands)]

    def ahead(tile, beyond, reach):
        mixed = tile if beyond is None else jnp.where(lane >= reach, tile, beyond)
        return tile + pltpu.roll(mixed, 128 - reach, 1)

    def behind(tile, before, reach):
        mixed = tile if before is None else jnp.where(lane < 128 - reach, tile, before)
        return tile + pltpu.roll(mixed, reach, 1)

    def three(west, own, east, reach, last):
        return ahead(west, own, reach), ahead(own, east, reach), None if last else ahead(east, None, reach)

    def two(west, own, reach, last):
        return None if last else behind(west, None, reach), behind(own, west, reach)

    def evaluate(scale, first, second, band, side):
        eps = eps_ref[scale, band]
        apart = first - second
        t0, t1, td = first * first + eps, second * second + eps, apart * apart + eps
        r0, r1, rd = lax.rsqrt(t0), lax.rsqrt(t1), lax.rsqrt(td)
        away = apart * rd
        cot_ref[scale, 0, side, band] = (first * r0 - away) * grad_scale[scale]
        cot_ref[scale, 1, side, band] = (second * r1 + away) * grad_scale[scale]
        return t0 * r0 + t1 * r1 - td * rd

    def channel(c, total):
        fields = []
        for m in range(2):
            fields.append(
                [
                    [ref[(m * bands + b - FIRST_PLANE) % peers, c + skip] * weight_ref[b] for b in range(bands)]
                    for ref, skip in ((west_ref, 0), (own_ref, start), (east_ref, 0))
                ]
            )
        for scale in range(LEVELS + 1):
            reach, part = 2**scale, None
            if scale < LEVELS:
                summed = [[rows_ahead(field, reach) if reach < 8 * bands else field for field in fields[m]] for m in range(2)]
                ahead_of = [([], [], []), ([], [], [])]
            for b in range(bands):
                if scale < LEVELS:
                    for m in range(2):
                        for side, tile in enumerate(three(*(field[b] for field in summed[m]), reach, scale == LEVELS - 1)):
                            ahead_of[m][side].append(tile)
                for side in range(2):
                    term = evaluate(scale, fields[0][side][b], fields[1][side][b], b, side)
                    part = term if part is None else part + term
            fields = ahead_of
            total = total + part * loss_scale[scale]
        for m in range(2):
            adjoint = [[cot_ref[LEVELS, m, side, b] for b in range(bands)] for side in range(2)]
            for level in reversed(range(LEVELS)):
                reach = 2**level
                if reach < 8 * bands:
                    adjoint = [rows_behind(field, reach) for field in adjoint]
                west, own = zip(*(two(adjoint[0][b], adjoint[1][b], reach, level == 0) for b in range(bands)))
                if level:
                    west = [west[b] + cot_ref[level, m, 0, b] for b in range(bands)]
                own = [own[b] + cot_ref[level, m, 1, b] for b in range(bands)]
                adjoint = [west, own]
            for b in range(bands):
                grad_ref[(m * bands + b - FIRST_PLANE) % peers, c + start] = adjoint[1][b] * weight_ref[b]
        return total

    me = lax.axis_index("mem") * lax.axis_size("lat") + lax.axis_index("lat")
    place = lax.rem(me + (peers - FIRST_PLANE), peers)
    count = jnp.clip(channels - place * share - start, 0, group)
    total = lax.fori_loop(0, count, channel, zero if start == 0 else refs[0][0, share])
    if final:
        term_ref[...] = jnp.broadcast_to(jnp.sum(total, axis=0).reshape(1, 1, 128), term_ref.shape)
    else:
        grad_ref[0, share] = total


def add_kernel(terms_ref, _, grad_ref):
    total = jnp.sum(terms_ref[...], axis=0)
    share = grad_ref.shape[1] - 1
    for p in range(grad_ref.shape[0]):
        grad_ref[p, share, 0:1] = total


def end_kernel(back_ref, gradient_ref, loss_ref, sum_ref, sems):
    peers, share, channels = back_ref.shape[0], back_ref.shape[1] - 1, gradient_ref.shape[0]
    copies = []
    for p in range(peers):
        size = min(share, channels - p * share)
        if size > 0:
            copies.append(
                pltpu.make_async_copy(
                    back_ref.at[p, pl.ds(0, size)], gradient_ref.at[pl.ds(p * share, size)], sems.at[p]
                )
            )
    for copy in copies:
        copy.start()
    total = back_ref[0, share, 0:1]
    for p in range(1, peers):
        total = total + back_ref[p, share, 0:1]
    sum_ref[...] = jnp.broadcast_to(jnp.sum(total, axis=1, keepdims=True), sum_ref.shape)
    copies.append(pltpu.make_async_copy(sum_ref, loss_ref, sems.at[peers]))
    copies[-1].start()
    for copy in copies:
        copy.wait()


def shards(members, target):
    channels, row_count, col_count = target.shape
    bands = lax.axis_size("lat")
    peers = lax.axis_size("mem") * bands
    nlat, nlon = row_count * bands, col_count * lax.axis_size("z") * lax.axis_size("core")
    share = -(-channels // peers)
    boxes = box_vectors(nlat)
    totals = [float(np.sum(vector, dtype=np.float64)) for vector in boxes]
    loss_scale = [0.5 / (2.0**s * channels * nlon * totals[s]) for s in range(LEVELS + 1)]
    grad_scale = [0.5 * nlat / (2.0**s * totals[s]) for s in range(LEVELS + 1)]
    table = np.zeros((bands, 8, 128), np.float32)
    for s in range(LEVELS + 1):
        table[:, :, s] = ((np.float32(2.0**s * EPS) * boxes[s]) ** 2).reshape(bands, 8)
    table[:, :, LEVELS + 1] = boxes[0].reshape(bands, 8)

    apart = jnp.pad(members[0] - target, ((0, peers * share - channels), (0, 0), (0, 0)))
    own = spread(apart, PLANE, FIRST_PLANE).reshape(peers, share, row_count, col_count)
    vmem = pl.BlockSpec(memory_space=pltpu.VMEM)
    shapes = [
        jax.ShapeDtypeStruct((peers, share + 1, row_count, col_count), jnp.float32),
        jax.ShapeDtypeStruct((lax.axis_size("z"), 1, col_count), jnp.float32),
    ]
    grad = None
    halos = []
    start = 0
    for size in GROUPS:
        part = own[:, start : start + size]
        halos.append((start, size, neighbour(part, 1), neighbour(part, -1)))
        start += size
    for start, size, west, east in halos:
        grad, *term = pl.pallas_call(
            functools.partial(box_kernel, loss_scale, grad_scale, channels, start, start + size == share),
            out_shape=shapes if start + size == share else shapes[:1],
            in_specs=[vmem] * (4 if start == 0 else 5),
            out_specs=[vmem] * (2 if start + size == share else 1),
            input_output_aliases={} if start == 0 else {4: 0},
            scratch_shapes=[
                pltpu.VMEM((LEVELS + 1, bands, 8, 128), jnp.float32),
                pltpu.VMEM((bands, 8, 128), jnp.float32),
                pltpu.VMEM((LEVELS + 1, 2, 2, bands, 8, 128), jnp.float32),
            ],
            compiler_params=pltpu.CompilerParams(vmem_limit_bytes=16 << 20),
            name=f"boxes_{start}",
        )(west, own, east, jnp.asarray(table), *(() if start == 0 else (grad,)))
    terms = spread(term[0], ("z",), FIRST_Z)
    grad = pl.pallas_call(
        add_kernel,
        out_shape=jax.ShapeDtypeStruct(grad.shape, jnp.float32),
        in_specs=[vmem, vmem],
        out_specs=vmem,
        input_output_aliases={1: 0},
        compiler_params=pltpu.CompilerParams(vmem_limit_bytes=4 << 20),
        name="add_terms",
    )(terms, grad)
    back = spread(grad, PLANE, FIRST_PLANE)
    gradient, loss = pl.pallas_call(
        end_kernel,
        out_shape=(
            jax.ShapeDtypeStruct((channels, row_count, col_count), jnp.float32),
            jax.ShapeDtypeStruct((1, 128), jnp.float32),
        ),
        in_specs=[vmem],
        out_specs=(pl.BlockSpec(memory_space=pl.ANY), pl.BlockSpec(memory_space=pl.ANY)),
        scratch_shapes=[pltpu.VMEM((1, 128), jnp.float32), pltpu.SemaphoreType.DMA((peers + 1,))],
        compiler_params=pltpu.CompilerParams(vmem_limit_bytes=4 << 20),
        name="end",
    )(back)
    return gradient[None], loss[0, 0]


def solution(mesh):
    grid = mesh.devices
    fine = Mesh(grid.reshape(*grid.shape[:2], grid.shape[2] // 2, 2), ("mem", "lat", "z", "core"))
    spec = P("mem", None, "lat", LON)
    return jax.shard_map(
        shards,
        mesh=fine,
        in_specs=(spec, P(None, "lat", LON)),
        out_specs=(spec, P()),
        check_vma=False,
    )
```

```python
import functools
import math

import jax
import jax.numpy as jnp
import numpy as np
from jax import lax
from jax.experimental import pallas as pl
from jax.experimental.pallas import tpu as pltpu
from jax.sharding import Mesh, PartitionSpec as P

LEVELS = 7
EPS = 0.05
GROUPS = (6,)
FIRST_PLANE = 14
FIRST_Z = 8
PLANE = ("mem", "lat")
LON = ("z", "core")


def box_vectors(row_count):
    row_index = np.arange(row_count, dtype=np.float32)
    degrees = np.float32(89.875) - np.float32(0.25) * row_index
    current = np.cos(degrees * np.float32(np.pi / 180.0)).astype(np.float32)
    boxes = [current]
    for level in range(LEVELS):
        reach = 2**level
        shifted = np.zeros_like(current)
        shifted[: max(row_count - reach, 0)] = current[reach:]
        current = current + shifted
        boxes.append(current)
    return boxes


def neighbour(value, by):
    count = lax.axis_size("z") * lax.axis_size("core")
    pairs = [(i, (i + by) % count) for i in range(count)]
    return lax.ppermute(value, LON, pairs)


def turned(count, first):
    return [(first + i) % count for i in range(count)]


def spread(value, axes, first):
    order = turned(math.prod(lax.axis_size(axis) for axis in axes), first)
    axes = axes if len(axes) > 1 else axes[0]
    return lax.all_to_all(value, axes, 0, 0, axis_index_groups=[order] if first else None, tiled=True)


def box_kernel(loss_scale, grad_scale, channels, start, final, west_ref, own_ref, east_ref, table_ref, *refs):
    eps_ref, weight_ref, cot_ref = refs[-3:]
    grad_ref, term_ref = refs[-5:-3] if final else (refs[-4], None)
    peers, share, group = own_ref.shape[0], own_ref.shape[1], west_ref.shape[1]
    bands = peers // 2
    for b in range(bands):
        table = table_ref[b]
        for scale in range(LEVELS + 1):
            eps_ref[scale, b] = jnp.broadcast_to(table[:, scale : scale + 1], (8, 128))
        weight_ref[b] = jnp.broadcast_to(table[:, LEVELS + 1 : LEVELS + 2], (8, 128))
    lane = lax.broadcasted_iota(jnp.int32, (8, 128), 1)
    row = lax.broadcasted_iota(jnp.int32, (8, 128), 0)
    zero = jnp.zeros((8, 128), jnp.float32)

    def rows_ahead(field, reach):
        if reach >= 8:
            hop = reach // 8
            return [field[b] + field[b + hop] if b + hop < bands else field[b] for b in range(bands)]
        rolled = [pltpu.roll(tile, 8 - reach, 0) for tile in field] + [zero]
        return [field[b] + jnp.where(row < 8 - reach, rolled[b], rolled[b + 1]) for b in range(bands)]

    def rows_behind(field, reach):
        if reach >= 8:
            hop = reach // 8
            return [field[b] + field[b - hop] if b >= hop else field[b] for b in range(bands)]
        rolled = [pltpu.roll(tile, reach, 0) for tile in field]
        before = [zero] + rolled[:-1]
        return [field[b] + jnp.where(row >= reach, rolled[b], before[b]) for b in range(bands)]

    def ahead(tile, beyond, reach):
        mixed = tile if beyond is None else jnp.where(lane >= reach, tile, beyond)
        return tile + pltpu.roll(mixed, 128 - reach, 1)

    def behind(tile, before, reach):
        mixed = tile if before is None else jnp.where(lane < 128 - reach, tile, before)
        return tile + pltpu.roll(mixed, reach, 1)

    def three(west, own, east, reach, last):
        return ahead(west, own, reach), ahead(own, east, reach), None if last else ahead(east, None, reach)

    def two(west, own, reach, last):
        return None if last else behind(west, None, reach), behind(own, west, reach)

    def evaluate(scale, first, second, band, side):
        eps = eps_ref[scale, band]
        apart = first - second
        t0, t1, td = first * first + eps, second * second + eps, apart * apart + eps
        r0, r1, rd = lax.rsqrt(t0), lax.rsqrt(t1), lax.rsqrt(td)
        away = apart * rd
        cot_ref[scale, 0, side, band] = (first * r0 - away) * grad_scale[scale]
        cot_ref[scale, 1, side, band] = (second * r1 + away) * grad_scale[scale]
        return t0 * r0 + t1 * r1 - td * rd

    def channel(c, total):
        fields = []
        for m in range(2):
            fields.append(
                [
                    [ref[(m * bands + b - FIRST_PLANE) % peers, c + skip] * weight_ref[b] for b in range(bands)]
                    for ref, skip in ((west_ref, 0), (own_ref, start), (east_ref, 0))
                ]
            )
        for scale in range(LEVELS + 1):
            reach, part = 2**scale, None
            if scale < LEVELS:
                summed = [[rows_ahead(field, reach) if reach < 8 * bands else field for field in fields[m]] for m in range(2)]
                ahead_of = [([], [], []), ([], [], [])]
            for b in range(bands):
                if scale < LEVELS:
                    for m in range(2):
                        for side, tile in enumerate(three(*(field[b] for field in summed[m]), reach, scale == LEVELS - 1)):
                            ahead_of[m][side].append(tile)
                for side in range(2):
                    term = evaluate(scale, fields[0][side][b], fields[1][side][b], b, side)
                    part = term if part is None else part + term
            fields = ahead_of
            total = total + part * loss_scale[scale]
        for m in range(2):
            adjoint = [[cot_ref[LEVELS, m, side, b] for b in range(bands)] for side in range(2)]
            for level in reversed(range(LEVELS)):
                reach = 2**level
                if reach < 8 * bands:
                    adjoint = [rows_behind(field, reach) for field in adjoint]
                west, own = zip(*(two(adjoint[0][b], adjoint[1][b], reach, level == 0) for b in range(bands)))
                if level:
                    west = [west[b] + cot_ref[level, m, 0, b] for b in range(bands)]
                own = [own[b] + cot_ref[level, m, 1, b] for b in range(bands)]
                adjoint = [west, own]
            for b in range(bands):
                grad_ref[(m * bands + b - FIRST_PLANE) % peers, c + start] = adjoint[1][b] * weight_ref[b]
        return total

    me = lax.axis_index("mem") * lax.axis_size("lat") + lax.axis_index("lat")
    place = lax.rem(me + (peers - FIRST_PLANE), peers)
    count = jnp.clip(channels - place * share - start, 0, group)
    total = lax.fori_loop(0, count, channel, zero if start == 0 else refs[0][0, share])
    if final:
        term_ref[...] = jnp.broadcast_to(jnp.sum(total, axis=0).reshape(1, 1, 128), term_ref.shape)
    else:
        grad_ref[0, share] = total


def add_kernel(terms_ref, _, grad_ref):
    total = jnp.sum(terms_ref[...], axis=0)
    share = grad_ref.shape[1] - 1
    for p in range(grad_ref.shape[0]):
        grad_ref[p, share, 0:1] = total


def end_kernel(back_ref, gradient_ref, loss_ref, sum_ref, sems):
    peers, share, channels = back_ref.shape[0], back_ref.shape[1] - 1, gradient_ref.shape[0]
    copies = []
    for p in range(peers):
        size = min(share, channels - p * share)
        if size > 0:
            copies.append(
                pltpu.make_async_copy(
                    back_ref.at[p, pl.ds(0, size)], gradient_ref.at[pl.ds(p * share, size)], sems.at[p]
                )
            )
    for copy in copies:
        copy.start()
    total = back_ref[0, share, 0:1]
    for p in range(1, peers):
        total = total + back_ref[p, share, 0:1]
    sum_ref[...] = jnp.broadcast_to(jnp.sum(total, axis=1, keepdims=True), sum_ref.shape)
    copies.append(pltpu.make_async_copy(sum_ref, loss_ref, sems.at[peers]))
    copies[-1].start()
    for copy in copies:
        copy.wait()


def shards(members, target):
    channels, row_count, col_count = target.shape
    bands = lax.axis_size("lat")
    peers = lax.axis_size("mem") * bands
    nlat, nlon = row_count * bands, col_count * lax.axis_size("z") * lax.axis_size("core")
    share = -(-channels // peers)
    boxes = box_vectors(nlat)
    totals = [float(np.sum(vector, dtype=np.float64)) for vector in boxes]
    loss_scale = [0.5 / (2.0**s * channels * nlon * totals[s]) for s in range(LEVELS + 1)]
    grad_scale = [0.5 * nlat / (2.0**s * totals[s]) for s in range(LEVELS + 1)]
    table = np.zeros((bands, 8, 128), np.float32)
    for s in range(LEVELS + 1):
        table[:, :, s] = ((np.float32(2.0**s * EPS) * boxes[s]) ** 2).reshape(bands, 8)
    table[:, :, LEVELS + 1] = boxes[0].reshape(bands, 8)

    apart = jnp.pad(members[0] - target, ((0, peers * share - channels), (0, 0), (0, 0)))
    own = spread(apart, PLANE, FIRST_PLANE).reshape(peers, share, row_count, col_count)
    vmem = pl.BlockSpec(memory_space=pltpu.VMEM)
    shapes = [
        jax.ShapeDtypeStruct((peers, share + 1, row_count, col_count), jnp.float32),
        jax.ShapeDtypeStruct((lax.axis_size("z"), 1, col_count), jnp.float32),
    ]
    grad = None
    halos = []
    start = 0
    for size in GROUPS:
        part = own[:, start : start + size]
        halos.append((start, size, neighbour(part, 1), neighbour(part, -1)))
        start += size
    for start, size, west, east in halos:
        grad, *term = pl.pallas_call(
            functools.partial(box_kernel, loss_scale, grad_scale, channels, start, start + size == share),
            out_shape=shapes if start + size == share else shapes[:1],
            in_specs=[vmem] * (4 if start == 0 else 5),
            out_specs=[vmem] * (2 if start + size == share else 1),
            input_output_aliases={} if start == 0 else {4: 0},
            scratch_shapes=[
                pltpu.VMEM((LEVELS + 1, bands, 8, 128), jnp.float32),
                pltpu.VMEM((bands, 8, 128), jnp.float32),
                pltpu.VMEM((LEVELS + 1, 2, 2, bands, 8, 128), jnp.float32),
            ],
            compiler_params=pltpu.CompilerParams(vmem_limit_bytes=16 << 20),
            name=f"boxes_{start}",
        )(west, own, east, jnp.asarray(table), *(() if start == 0 else (grad,)))
    terms = spread(term[0], ("z",), FIRST_Z)
    grad = pl.pallas_call(
        add_kernel,
        out_shape=jax.ShapeDtypeStruct(grad.shape, jnp.float32),
        in_specs=[vmem, vmem],
        out_specs=vmem,
        input_output_aliases={1: 0},
        compiler_params=pltpu.CompilerParams(vmem_limit_bytes=4 << 20),
        name="add_terms",
    )(terms, grad)
    back = spread(grad, PLANE, FIRST_PLANE)
    gradient, loss = pl.pallas_call(
        end_kernel,
        out_shape=(
            jax.ShapeDtypeStruct((channels, row_count, col_count), jnp.float32),
            jax.ShapeDtypeStruct((1, 128), jnp.float32),
        ),
        in_specs=[vmem],
        out_specs=(pl.BlockSpec(memory_space=pl.ANY), pl.BlockSpec(memory_space=pl.ANY)),
        scratch_shapes=[pltpu.VMEM((1, 128), jnp.float32), pltpu.SemaphoreType.DMA((peers + 1,))],
        compiler_params=pltpu.CompilerParams(vmem_limit_bytes=4 << 20),
        name="end",
    )(back)
    return gradient[None], loss[0, 0]


def solution(mesh):
    grid = mesh.devices
    fine = Mesh(grid.reshape(*grid.shape[:2], grid.shape[2] // 2, 2), ("mem", "lat", "z", "core"))
    spec = P("mem", None, "lat", LON)
    return jax.shard_map(
        shards,
        mesh=fine,
        in_specs=(spec, P(None, "lat", LON)),
        out_specs=(spec, P()),
        check_vma=False,
    )
```
